32 devices in a mesh: wide: 16 (over z, y, x), narrow: 2 (over core).
Axes of the slice: x: 2, y: 2, z: 4, core: 2. Of those that a mesh axis runs over, the one named last changes fastest.
Arguments:
- samples: float32 [128, 32768], P('narrow', 'wide'), may hold values from -6 to 6
- row_weights: float32 [4096], P('narrow'), may hold values from 0.1 to 10
- tile_ranks: int32 [8, 64], P('narrow', 'wide'), may hold values from 16 to 80, as said below
- u_factors: bfloat16 [8, 64, 80, 512], P('narrow', 'wide'), may hold values from -0.125 to 0.125
- v_factors: bfloat16 [8, 64, 80, 512], P('narrow', 'wide'), may hold values from -0.25 to 0.25
Outputs:
- forward_rows: float32 [128, 4096], P('wide', 'narrow')
- adjoint_cols: float32 [128, 32768], P(None, ('wide', 'narrow'))
The draws below stay inside these ranges and needn't reach their ends.
Inputs may be any that keep to these rules, and one draw needn't show every extreme that they name: `tile_ranks`: every rank is a multiple of 16.
All inputs are finite; a program needn't handle non-finite values.
Results may differ from the reference program's by a relative error of at most 0.0085.
Values may be sent and summed in bfloat16 or wider, within the bound.
A program may use at most 64 MiB of HBM per device.

```python
import math
import jax
import jax.numpy as jnp
from jax import lax

B = 512
RMAX = 80
S = 128
TILE_ROWS = 8
TILE_COLS = 64
ORDER_ROWS = 4096
ORDER_COLS = 32768


def draw_tile_ranks(key, part):
    steps = RMAX // 16
    base = jax.random.randint(jax.random.fold_in(key, 11), (TILE_ROWS, TILE_COLS), 1, steps + 1)
    offset = jax.random.randint(jax.random.fold_in(key, 13), (), 0, TILE_COLS)
    row_ids = jnp.arange(TILE_ROWS, dtype=jnp.int32)[:, None]
    col_ids = jnp.arange(TILE_COLS, dtype=jnp.int32)[None, :]
    centre = (row_ids * TILE_COLS // TILE_ROWS + offset) % TILE_COLS
    apart = (col_ids - centre) % TILE_COLS
    near_band = (apart <= 1) | (apart >= TILE_COLS - 1)
    levels = jnp.where(near_band, steps, base)
    lowest_col = (offset + TILE_COLS // 2) % TILE_COLS
    lowest = (row_ids == 0) & (col_ids == lowest_col)
    levels = jnp.where(lowest, 1, levels)
    return (16 * levels).astype(jnp.int32)


def level_of(own_key, extent, cuts, smallest, top_value):
    level, own = 1.0, jax.random.fold_in(own_key, 6)
    for axis_at, blocks in cuts:
        draws = jnp.exp(jax.random.uniform(jax.random.fold_in(own, axis_at), (blocks,), jnp.float32, smallest / len(cuts), top_value / len(cuts)))
        level = level * jnp.repeat(draws, extent[axis_at] // blocks).reshape([-1 if axis == axis_at else 1 for axis in range(len(extent))])
    return level


def noise(rng, shape, scale, reach, pieces=(), kind=jnp.bfloat16):
    result = jax.random.normal(rng, shape, jnp.float32) * scale
    if len(pieces) > 0:
        result = level_of(rng, shape, pieces, -0.22, 0.18) * result
    return jnp.clip(result, min=-reach, max=reach).astype(kind)


def setup_inputs(seed: int = 0) -> dict:
    arg_keys = jax.random.split(jax.random.key(seed), 6)
    return {
        "samples": noise(arg_keys[0], (S, ORDER_COLS), 1.0, 6.0, ((0, 2), (1, 16)), jnp.float32),
        "row_weights": jnp.clip(jnp.exp(math.log(10.0) - 4.6051702 * jax.random.uniform(arg_keys[1], (ORDER_ROWS,), jnp.float32) ** level_of(arg_keys[1], (ORDER_ROWS,), ((0, 2),), -0.2, 0.2)), 0.1, 10.0),
        "tile_ranks": draw_tile_ranks(jax.random.fold_in(arg_keys[5], 71), 0),
        "u_factors": noise(arg_keys[3], (TILE_ROWS, TILE_COLS, RMAX, B), (RMAX * TILE_COLS // 2) ** -0.5, 0.125, ((0, 2), (1, 16))),
        "v_factors": noise(arg_keys[4], (TILE_ROWS, TILE_COLS, RMAX, B), B ** -0.5, 0.25, ((0, 2), (1, 16))),
    }


def reference(samples, row_weights, tile_ranks, u_factors, v_factors):
    tile_rows, tile_cols, rank_cap, tile_size = v_factors.shape
    col_count = samples.shape[0]
    levels = jnp.arange(rank_cap, dtype=jnp.int32)
    rank_mask = (levels[None, None, :] < tile_ranks[:, :, None]).astype(jnp.float32)
    columns = samples.astype(jnp.bfloat16).astype(jnp.float32).reshape(col_count, tile_cols, tile_size)
    highest = lax.Precision.HIGHEST

    def forward(tile_index):
        v_block = lax.dynamic_index_in_dim(v_factors, tile_index, 0, keepdims=False).astype(jnp.float32)
        u_block = lax.dynamic_index_in_dim(u_factors, tile_index, 0, keepdims=False).astype(jnp.float32)
        row_mask = lax.dynamic_index_in_dim(rank_mask, tile_index, 0, keepdims=False)
        coeffs = jnp.einsum("sjb,jrb->jrs", columns, v_block, precision=highest) * row_mask[:, :, None]
        coeffs = coeffs.astype(jnp.bfloat16).astype(jnp.float32)
        return jnp.einsum("jrs,jrb->sb", coeffs, u_block, precision=highest)

    row_blocks = lax.map(forward, jnp.arange(tile_rows, dtype=jnp.int32))
    row_total = jnp.transpose(row_blocks, (1, 0, 2)).reshape(col_count, tile_rows * tile_size)
    weighted = (row_total * row_weights[None, :]).astype(jnp.bfloat16).astype(jnp.float32)
    weighted = weighted.reshape(col_count, tile_rows, tile_size)

    def adjoint(tile_index):
        u_block = lax.dynamic_index_in_dim(u_factors, tile_index, 1, keepdims=False).astype(jnp.float32)
        v_block = lax.dynamic_index_in_dim(v_factors, tile_index, 1, keepdims=False).astype(jnp.float32)
        col_mask = lax.dynamic_index_in_dim(rank_mask, tile_index, 1, keepdims=False)
        adjoint_coeffs = jnp.einsum("sib,irb->irs", weighted, u_block, precision=highest) * col_mask[:, :, None]
        adjoint_coeffs = adjoint_coeffs.astype(jnp.bfloat16).astype(jnp.float32)
        return jnp.einsum("irs,irb->sb", adjoint_coeffs, v_block, precision=highest)

    col_blocks = lax.map(adjoint, jnp.arange(tile_cols, dtype=jnp.int32))
    col_total = jnp.transpose(col_blocks, (1, 0, 2)).reshape(col_count, tile_cols * tile_size)
    return row_total, col_total
```

```python
import functools
import jax
import jax.numpy as jnp
from jax import lax
from jax.experimental import pallas as pl
from jax.experimental.pallas import tpu as pltpu
from jax.sharding import PartitionSpec as P

MESH = pl.DeviceIdType.MESH
NT = (((1,), (1,)), ((), ()))
NN = (((1,), (0,)), ((), ()))
F32 = jnp.float32
BF16 = jnp.bfloat16


def plane_size(wide):
    size = 1
    while size * 2 * size * 2 <= wide and wide % (size * 2) == 0:
        size *= 2
    return size


def kernel(
    nz, np_, nn,
    ranks_ref, rw_ref, x_ref, u_hbm, v_hbm, fwd_ref, adj_ref,
    xg, u, v, part, sendbuf, recv1, own2, send2, recv2, gath, back, bsend, brecv, back_out,
    in_sems, xs, xr, s1, q1, s2, q2, s3, q3, s4, q4, s5, q5,
):
    ni, nj, rank_cap, tile = u.shape
    own_rows = xg.shape[1]
    cols = xg.shape[0] * own_rows
    share = recv2.shape[-2]
    width = bsend.shape[-1]
    w = lax.axis_index("wide")
    n = lax.axis_index("narrow")
    p = lax.rem(w, np_)
    z = lax.div(w, np_)

    loads = []
    for i in range(ni):
        cv = pltpu.make_async_copy(v_hbm.at[i], v.at[i], in_sems.at[0, i])
        cu = pltpu.make_async_copy(u_hbm.at[i], u.at[i], in_sems.at[1, i])
        cv.start()
        cu.start()
        loads.append((cv, cu))

    plane_peers = [z * np_ + lax.rem(p + d, np_) for d in range(1, np_)]
    z_peers = [lax.rem(z + d, nz) * np_ + p for d in range(1, nz)]
    n_peers = [lax.rem(n + d, nn) for d in range(1, nn)]

    barrier = pltpu.get_barrier_semaphore()
    for peer in plane_peers + z_peers:
        pl.semaphore_signal(barrier, inc=1, device_id=(peer, n), device_id_type=MESH)
    for peer in n_peers:
        pl.semaphore_signal(barrier, inc=1, device_id=(w, peer), device_id_type=MESH)
    xg[n] = x_ref[...].astype(BF16)
    pl.semaphore_wait(barrier, len(plane_peers) + len(z_peers) + len(n_peers))

    sends = []

    def send(src, dst, send_sem, recv_sem, device):
        copy = pltpu.make_async_remote_copy(
            src_ref=src, dst_ref=dst, send_sem=send_sem, recv_sem=recv_sem,
            device_id=device, device_id_type=MESH,
        )
        copy.start()
        sends.append(copy)
        return copy

    x_copies = [
        send(xg.at[n], xg.at[n], xs.at[d], xr.at[d], (w, peer)) for d, peer in enumerate(n_peers)
    ]
    for copy in x_copies:
        copy.wait_recv()

    lanes = lax.broadcasted_iota(jnp.int32, (cols, rank_cap), 1)

    def forward(i):
        for copy in loads[i]:
            copy.wait()
        total = jnp.zeros((cols, tile), F32)
        for j in range(nj):
            xj = xg[:, :, j * tile : (j + 1) * tile].reshape(cols, tile)
            c = lax.dot_general(xj, v[i, j], NT, preferred_element_type=F32)
            c = jnp.where(lanes < ranks_ref[i, j], c, 0.0).astype(BF16)
            total += lax.dot_general(c, u[i, j], NN, preferred_element_type=F32)
        total = total.reshape(nz, np_, share, tile)
        part[i] = total
        sendbuf[i] = total.astype(BF16)
        return [
            send(
                sendbuf.at[i, :, lax.rem(p + d + 1, np_)], recv1.at[i, d],
                s1.at[i, d], q1.at[i, d], (peer, n),
            )
            for d, peer in enumerate(plane_peers)
        ]

    def plane_sum(i, copies):
        for copy in copies:
            copy.wait_recv()
        total = part[i, :, p]
        for d in range(np_ - 1):
            total += recv1[i, d].astype(F32)
        own2[i] = total
        send2[i] = total.astype(BF16)
        return [
            send(
                send2.at[i, lax.rem(z + d + 1, nz)], recv2.at[i, d],
                s2.at[i, d], q2.at[i, d], (peer, n),
            )
            for d, peer in enumerate(z_peers)
        ]

    def z_sum(i, copies):
        for copy in copies:
            copy.wait_recv()
        total = own2[i, z]
        for d in range(nz - 1):
            total += recv2[i, d].astype(F32)
        fwd_ref[:, i * tile : (i + 1) * tile] = total
        rw = rw_ref[i * tile : (i + 1) * tile].reshape(1, tile)
        gath[i, z, p] = (total * rw).astype(BF16)
        return [
            send(
                gath.at[i, z, p], gath.at[i, z, p], s3.at[i, d], q3.at[i, d], (peer, n)
            )
            for d, peer in enumerate(z_peers)
        ]

    def spread(i, copies):
        for copy in copies:
            copy.wait_recv()
        return [
            send(gath.at[i, :, p], gath.at[i, :, p], s4.at[i, d], q4.at[i, d], (peer, n))
            for d, peer in enumerate(plane_peers)
        ]

    def adjoint(i, copies):
        for copy in copies:
            copy.wait_recv()
        wt = gath[i].astype(F32).reshape(cols, tile).astype(BF16)
        for j in range(nj):
            c = lax.dot_general(wt, u[i, j], NT, preferred_element_type=F32)
            c = jnp.where(lanes < ranks_ref[i, j], c, 0.0).astype(BF16)
            b = lax.dot_general(c, v[i, j], NN, preferred_element_type=F32)
            at = slice(j * tile, (j + 1) * tile)
            if i > 0:
                b += back[:, at]
            if i < ni - 1:
                back[:, at] = b
                continue
            step = min(width, tile)
            for k in range(tile // step):
                begin = j * tile + k * step
                m, off = begin // width, begin % width
                piece = b[:, k * step : (k + 1) * step]
                back_out[m, :, off : off + step] = piece
                bsend[m, :, off : off + step] = piece.astype(BF16)

    stage = {}
    lag = [(forward, 0), (plane_sum, ni), (z_sum, ni + 2), (spread, ni + 3), (adjoint, ni + 4)]
    plan = sorted(
        (start + i, -k, i) for k, (_, start) in enumerate(lag) for i in range(ni)
    )
    for _, k, i in plan:
        k = -k
        func = lag[k][0]
        if k == 0:
            stage[i] = func(i)
        else:
            stage[i] = func(i, stage[i])

    copies = [
        send(
            bsend.at[peer], brecv.at[d], s5.at[d], q5.at[d], (w, peer)
        )
        for d, peer in enumerate(n_peers)
    ]
    total = back_out[n]
    for d, copy in enumerate(copies):
        copy.wait_recv()
        total += brecv[d].astype(F32)
    adj_ref[...] = total
    for copy in sends:
        copy.wait_send()


def on_device(wide, nn, samples, row_weights, tile_ranks, u_factors, v_factors):
    ni, nj, rank_cap, tile = v_factors.shape
    own_rows, own_cols = samples.shape
    cols = own_rows * nn
    share = cols // wide
    np_ = plane_size(wide)
    nz = wide // np_
    width = own_cols // nn
    dma = pltpu.SemaphoreType.DMA
    vmem = pltpu.VMEM
    some = lambda k: max(k, 1)
    scratch = [
        vmem((nn, own_rows, own_cols), BF16),
        vmem(u_factors.shape, BF16),
        vmem(v_factors.shape, BF16),
        vmem((ni, nz, np_, share, tile), F32),
        vmem((ni, nz, np_, share, tile), BF16),
        vmem((ni, some(np_ - 1), nz, share, tile), BF16),
        vmem((ni, nz, share, tile), F32),
        vmem((ni, nz, share, tile), BF16),
        vmem((ni, some(nz - 1), share, tile), BF16),
        vmem((ni, nz, np_, share, tile), BF16),
        vmem((cols, own_cols), F32),
        vmem((nn, cols, width), BF16),
        vmem((some(nn - 1), cols, width), BF16),
        vmem((nn, cols, width), F32),
        dma((2, ni)),
        dma((some(nn - 1),)), dma((some(nn - 1),)),
        dma((ni, some(np_ - 1))), dma((ni, some(np_ - 1))),
        dma((ni, some(nz - 1))), dma((ni, some(nz - 1))),
        dma((ni, some(nz - 1))), dma((ni, some(nz - 1))),
        dma((ni, some(np_ - 1))), dma((ni, some(np_ - 1))),
        dma((some(nn - 1),)), dma((some(nn - 1),)),
    ]
    in_vmem = pl.BlockSpec(memory_space=pltpu.VMEM)
    return pl.pallas_call(
        functools.partial(kernel, nz, np_, nn),
        out_shape=(
            jax.ShapeDtypeStruct((share, ni * tile), F32),
            jax.ShapeDtypeStruct((cols, width), F32),
        ),
        in_specs=[
            pl.BlockSpec(memory_space=pltpu.SMEM), in_vmem, in_vmem,
            pl.BlockSpec(memory_space=pl.ANY), pl.BlockSpec(memory_space=pl.ANY),
        ],
        out_specs=(in_vmem, in_vmem),
        scratch_shapes=scratch,
        compiler_params=pltpu.CompilerParams(
            collective_id=0, has_side_effects=True, vmem_limit_bytes=56 << 20
        ),
        name="operator",
    )(tile_ranks, row_weights, samples, u_factors, v_factors)


def solution(mesh):
    in_specs = (
        P("narrow", "wide"),
        P("narrow"),
        P("narrow", "wide"),
        P("narrow", "wide", None, None),
        P("narrow", "wide", None, None),
    )
    out_specs = (P("wide", "narrow"), P(None, ("wide", "narrow")))
    body = functools.partial(on_device, mesh.shape["wide"], mesh.shape["narrow"])
    return jax.shard_map(
        body, mesh=mesh, in_specs=in_specs, out_specs=out_specs, check_vma=False
    )
```

```python
import functools
import jax
import jax.numpy as jnp
from jax import lax
from jax.experimental import pallas as pl
from jax.experimental.pallas import tpu as pltpu
from jax.sharding import PartitionSpec as P

MESH = pl.DeviceIdType.MESH
NT = (((1,), (1,)), ((), ()))
NN = (((1,), (0,)), ((), ()))
F32 = jnp.float32
BF16 = jnp.bfloat16


def plane_size(wide):
    size = 1
    while size * 2 * size * 2 <= wide and wide % (size * 2) == 0:
        size *= 2
    return size


def kernel(
    nz, np_, nn,
    ranks_ref, rw_ref, x_hbm, u_hbm, v_hbm, fwd_ref, adj_ref,
    xg, u, v, part, sendbuf, recv1, own2, send2, recv2, gath, back, bsend, brecv, back_out, x_in,
    x_sem, in_sems, xs, xr, s1, q1, s2, q2, s3, q3, s4, q4, s5, q5,
):
    ni, nj, rank_cap, tile = u.shape
    own_rows = xg.shape[1]
    cols = xg.shape[0] * own_rows
    share = recv2.shape[-2]
    width = bsend.shape[-1]
    w = lax.axis_index("wide")
    n = lax.axis_index("narrow")
    p = lax.rem(w, np_)
    z = lax.div(w, np_)

    plane_peers = [z * np_ + lax.rem(p + d, np_) for d in range(1, np_)]
    z_peers = [lax.rem(z + d, nz) * np_ + p for d in range(1, nz)]
    n_peers = [lax.rem(n + d, nn) for d in range(1, nn)]

    barrier = pltpu.get_barrier_semaphore()
    for peer in plane_peers + z_peers:
        pl.semaphore_signal(barrier, inc=1, device_id=(peer, n), device_id_type=MESH)
    for peer in n_peers:
        pl.semaphore_signal(barrier, inc=1, device_id=(w, peer), device_id_type=MESH)
    x_load = pltpu.make_async_copy(x_hbm, x_in, x_sem)
    x_load.start()
    loads = []
    for i in range(ni):
        cv = pltpu.make_async_copy(v_hbm.at[i], v.at[i], in_sems.at[0, i])
        cu = pltpu.make_async_copy(u_hbm.at[i], u.at[i], in_sems.at[1, i])
        cv.start()
        cu.start()
        loads.append((cv, cu))

    x_load.wait()
    xg[n] = x_in[...].astype(BF16)
    pl.semaphore_wait(barrier, len(plane_peers) + len(z_peers) + len(n_peers))

    sends = []

    def send(src, dst, send_sem, recv_sem, device):
        copy = pltpu.make_async_remote_copy(
            src_ref=src, dst_ref=dst, send_sem=send_sem, recv_sem=recv_sem,
            device_id=device, device_id_type=MESH,
        )
        copy.start()
        sends.append(copy)
        return copy

    x_copies = [
        send(xg.at[n], xg.at[n], xs.at[d], xr.at[d], (w, peer)) for d, peer in enumerate(n_peers)
    ]
    for copy in x_copies:
        copy.wait_recv()

    lanes = lax.broadcasted_iota(jnp.int32, (cols, rank_cap), 1)

    def forward(i):
        for copy in loads[i]:
            copy.wait()
        total = jnp.zeros((cols, tile), F32)
        for j in range(nj):
            xj = xg[:, :, j * tile : (j + 1) * tile].reshape(cols, tile)
            c = lax.dot_general(xj, v[i, j], NT, preferred_element_type=F32)
            c = jnp.where(lanes < ranks_ref[i, j], c, 0.0).astype(BF16)
            total += lax.dot_general(c, u[i, j], NN, preferred_element_type=F32)
        total = total.reshape(nz, np_, share, tile)
        part[i] = total
        sendbuf[i] = total.astype(BF16)
        return [
            send(
                sendbuf.at[i, :, lax.rem(p + d + 1, np_)], recv1.at[i, d],
                s1.at[i, d], q1.at[i, d], (peer, n),
            )
            for d, peer in enumerate(plane_peers)
        ]

    def plane_sum(i, copies):
        for copy in copies:
            copy.wait_recv()
        total = part[i, :, p]
        for d in range(np_ - 1):
            total += recv1[i, d].astype(F32)
        own2[i] = total
        send2[i] = total.astype(BF16)
        return [
            send(
                send2.at[i, lax.rem(z + d + 1, nz)], recv2.at[i, d],
                s2.at[i, d], q2.at[i, d], (peer, n),
            )
            for d, peer in enumerate(z_peers)
        ]

    def z_sum(i, copies):
        for copy in copies:
            copy.wait_recv()
        total = own2[i, z]
        for d in range(nz - 1):
            total += recv2[i, d].astype(F32)
        fwd_ref[:, i * tile : (i + 1) * tile] = total
        rw = rw_ref[i * tile : (i + 1) * tile].reshape(1, tile)
        gath[i, z, p] = (total * rw).astype(BF16)
        return [
            send(
                gath.at[i, z, p], gath.at[i, z, p], s3.at[i, d], q3.at[i, d], (peer, n)
            )
            for d, peer in enumerate(z_peers)
        ]

    def spread(i, copies):
        for copy in copies:
            copy.wait_recv()
        return [
            send(gath.at[i, :, p], gath.at[i, :, p], s4.at[i, d], q4.at[i, d], (peer, n))
            for d, peer in enumerate(plane_peers)
        ]

    def adjoint(i, copies):
        for copy in copies:
            copy.wait_recv()
        wt = gath[i].astype(F32).reshape(cols, tile).astype(BF16)
        for j in range(nj):
            c = lax.dot_general(wt, u[i, j], NT, preferred_element_type=F32)
            c = jnp.where(lanes < ranks_ref[i, j], c, 0.0).astype(BF16)
            b = lax.dot_general(c, v[i, j], NN, preferred_element_type=F32)
            at = slice(j * tile, (j + 1) * tile)
            if i > 0:
                b += back[:, at]
            if i < ni - 1:
                back[:, at] = b
                continue
            step = min(width, tile)
            for k in range(tile // step):
                begin = j * tile + k * step
                m, off = begin // width, begin % width
                piece = b[:, k * step : (k + 1) * step]
                back_out[m, :, off : off + step] = piece
                bsend[m, :, off : off + step] = piece.astype(BF16)

    stage = {}
    lag = [(forward, 0), (plane_sum, ni), (z_sum, 2 * ni), (spread, 3 * ni), (adjoint, 4 * ni)]
    plan = sorted(
        (start + i, -k, i) for k, (_, start) in enumerate(lag) for i in range(ni)
    )
    for _, k, i in plan:
        k = -k
        func = lag[k][0]
        if k == 0:
            stage[i] = func(i)
        else:
            stage[i] = func(i, stage[i])

    copies = [
        send(
            bsend.at[peer], brecv.at[d], s5.at[d], q5.at[d], (w, peer)
        )
        for d, peer in enumerate(n_peers)
    ]
    total = back_out[n]
    for d, copy in enumerate(copies):
        copy.wait_recv()
        total += brecv[d].astype(F32)
    adj_ref[...] = total
    for copy in sends:
        copy.wait_send()


def on_device(wide, nn, samples, row_weights, tile_ranks, u_factors, v_factors):
    ni, nj, rank_cap, tile = v_factors.shape
    own_rows, own_cols = samples.shape
    cols = own_rows * nn
    share = cols // wide
    np_ = plane_size(wide)
    nz = wide // np_
    width = own_cols // nn
    dma = pltpu.SemaphoreType.DMA
    vmem = pltpu.VMEM
    some = lambda k: max(k, 1)
    scratch = [
        vmem((nn, own_rows, own_cols), BF16),
        vmem(u_factors.shape, BF16),
        vmem(v_factors.shape, BF16),
        vmem((ni, nz, np_, share, tile), F32),
        vmem((ni, nz, np_, share, tile), BF16),
        vmem((ni, some(np_ - 1), nz, share, tile), BF16),
        vmem((ni, nz, share, tile), F32),
        vmem((ni, nz, share, tile), BF16),
        vmem((ni, some(nz - 1), share, tile), BF16),
        vmem((ni, nz, np_, share, tile), BF16),
        vmem((cols, own_cols), F32),
        vmem((nn, cols, width), BF16),
        vmem((some(nn - 1), cols, width), BF16),
        vmem((nn, cols, width), F32),
        vmem(samples.shape, F32),
        dma(()),
        dma((2, ni)),
        dma((some(nn - 1),)), dma((some(nn - 1),)),
        dma((ni, some(np_ - 1))), dma((ni, some(np_ - 1))),
        dma((ni, some(nz - 1))), dma((ni, some(nz - 1))),
        dma((ni, some(nz - 1))), dma((ni, some(nz - 1))),
        dma((ni, some(np_ - 1))), dma((ni, some(np_ - 1))),
        dma((some(nn - 1),)), dma((some(nn - 1),)),
    ]
    in_vmem = pl.BlockSpec(memory_space=pltpu.VMEM)
    return pl.pallas_call(
        functools.partial(kernel, nz, np_, nn),
        out_shape=(
            pltpu.VMEM((share, ni * tile), F32),
            pltpu.VMEM((cols, width), F32),
        ),
        in_specs=[
            pl.BlockSpec(memory_space=pltpu.SMEM), in_vmem, pl.BlockSpec(memory_space=pl.ANY),
            pl.BlockSpec(memory_space=pl.ANY), pl.BlockSpec(memory_space=pl.ANY),
        ],
        out_specs=(in_vmem, in_vmem),
        scratch_shapes=scratch,
        compiler_params=pltpu.CompilerParams(
            collective_id=0, has_side_effects=True, vmem_limit_bytes=56 << 20
        ),
        name="operator",
    )(tile_ranks, row_weights, samples, u_factors, v_factors)


def solution(mesh):
    in_specs = (
        P("narrow", "wide"),
        P("narrow"),
        P("narrow", "wide"),
        P("narrow", "wide", None, None),
        P("narrow", "wide", None, None),
    )
    out_specs = (P("wide", "narrow"), P(None, ("wide", "narrow")))
    body = functools.partial(on_device, mesh.shape["wide"], mesh.shape["narrow"])
    return jax.shard_map(
        body, mesh=mesh, in_specs=in_specs, out_specs=out_specs, check_vma=False
    )
```

```python
import functools
import jax
import jax.numpy as jnp
from jax import lax
from jax.experimental import pallas as pl
from jax.experimental.pallas import tpu as pltpu
from jax.sharding import PartitionSpec as P

MESH = pl.DeviceIdType.MESH
NT = (((1,), (1,)), ((), ()))
NN = (((1,), (0,)), ((), ()))
F32 = jnp.float32
BF16 = jnp.bfloat16


def plane_size(wide):
    size = 1
    while size * 2 * size * 2 <= wide and wide % (size * 2) == 0:
        size *= 2
    return size


def flips(own, size):
    if size & (size - 1):
        return [lax.rem(own + d, size) for d in range(1, size)]
    out = []
    for d in range(size - 1, 0, -1):
        flipped = 0
        bit = 1
        while bit < size:
            digit = lax.rem(lax.div(own, bit), 2)
            flipped += bit * (1 - digit if d & bit else digit)
            bit *= 2
        out.append(flipped)
    return out


def kernel(
    schemes, nn,
    ranks_ref, rw_ref, x_hbm, u_hbm, v_hbm, fwd_ref, adj_ref,
    xg, u, v, back, bsend, brecv, back_out, x_in,
    x_sem, in_sems, xs, xr, s5, q5, *blocks,
):
    ni, nj, rank_cap, tile = u.shape
    each = len(blocks) // ni
    blocks = [blocks[i * each : (i + 1) * each] for i in range(ni)]
    own_rows = xg.shape[1]
    cols = xg.shape[0] * own_rows
    share = fwd_ref.shape[0]
    width = bsend.shape[-1]
    w = lax.axis_index("wide")
    n = lax.axis_index("narrow")

    rest, plane = schemes[0][:2]
    if schemes[0][2]:
        rest, plane = plane, rest
    at_z, at_p = lax.div(w, plane), lax.rem(w, plane)

    def axis_of(i, first):
        nz, np_, swapped = schemes[i]
        p, z = (at_z, at_p) if swapped else (at_p, at_z)
        if first != swapped:
            peers = [(at_z * plane + q, q) for q in flips(at_p, plane)]
        else:
            peers = [(q * plane + at_p, q) for q in flips(at_z, rest)]
        return nz, np_, p, z, peers

    w_peers = [q for q, _ in axis_of(0, True)[4] + axis_of(0, False)[4]]

    n_peers = [lax.rem(n + d, nn) for d in range(1, nn)]

    barrier = pltpu.get_barrier_semaphore()
    for peer in w_peers:
        pl.semaphore_signal(barrier, inc=1, device_id=(peer, n), device_id_type=MESH)
    for peer in n_peers:
        pl.semaphore_signal(barrier, inc=1, device_id=(w, peer), device_id_type=MESH)
    x_load = pltpu.make_async_copy(x_hbm, x_in, x_sem)
    x_load.start()
    loads = []
    for i in range(ni):
        cv = pltpu.make_async_copy(v_hbm.at[i], v.at[i], in_sems.at[0, i])
        cu = pltpu.make_async_copy(u_hbm.at[i], u.at[i], in_sems.at[1, i])
        cv.start()
        cu.start()
        loads.append((cv, cu))

    x_load.wait()
    xg[n] = x_in[...].astype(BF16)
    pl.semaphore_wait(barrier, len(w_peers) + len(n_peers))

    sends = []

    def send(src, dst, send_sem, recv_sem, device):
        copy = pltpu.make_async_remote_copy(
            src_ref=src, dst_ref=dst, send_sem=send_sem, recv_sem=recv_sem,
            device_id=device, device_id_type=MESH,
        )
        copy.start()
        sends.append(copy)
        return copy

    x_copies = [
        send(xg.at[n], xg.at[n], xs.at[d], xr.at[d], (w, peer)) for d, peer in enumerate(n_peers)
    ]
    for copy in x_copies:
        copy.wait_recv()

    lanes = lax.broadcasted_iota(jnp.int32, (cols, rank_cap), 1)

    def scatter(i):
        for copy in loads[i]:
            copy.wait()
        total = jnp.zeros((cols, tile), F32)
        for j in range(nj):
            xj = xg[:, :, j * tile : (j + 1) * tile].reshape(cols, tile)
            c = lax.dot_general(xj, v[i, j], NT, preferred_element_type=F32)
            c = jnp.where(lanes < ranks_ref[i, j], c, 0.0).astype(BF16)
            total += lax.dot_general(c, u[i, j], NN, preferred_element_type=F32)
        part, sendbuf, recv1 = blocks[i][:3]
        s1, q1 = blocks[i][7:9]
        nz, np_, p, z, peers = axis_of(i, True)
        total = total.reshape(rest, plane, share, tile)
        for q in range(np_):
            block = total[q] if schemes[i][2] else total[:, q]
            part[q] = block
            sendbuf[q] = block.astype(BF16)
        return [
            send(sendbuf.at[q], recv1.at[d], s1.at[d], q1.at[d], (peer, n))
            for d, (peer, q) in enumerate(peers)
        ]

    def plane_sum(i, copies):
        part, _, recv1, own2, send2, recv2 = blocks[i][:6]
        s2, q2 = blocks[i][9:11]
        nz, np_, p, z, _ = axis_of(i, True)
        for copy in copies:
            copy.wait_recv()
        total = part[p]
        for d in range(np_ - 1):
            total += recv1[d].astype(F32)
        own2[...] = total
        peers = axis_of(i, False)[4]
        if nz > 1:
            send2[...] = total.astype(BF16)
        return [
            send(
                send2.at[q], recv2.at[d], s2.at[d], q2.at[d], (peer, n)
            )
            for d, (peer, q) in enumerate(peers)
        ]

    def z_sum(i, copies):
        own2, _, recv2, gath = blocks[i][3:7]
        s3, q3 = blocks[i][11:13]
        nz, _, p, z, peers = axis_of(i, False)
        for copy in copies:
            copy.wait_recv()
        total = own2[z]
        for d in range(nz - 1):
            total += recv2[d].astype(F32)
        fwd_ref[:, i * tile : (i + 1) * tile] = total
        rw = rw_ref[i * tile : (i + 1) * tile].reshape(1, tile)
        gath[p, z] = (total * rw).astype(BF16)
        return [
            send(gath.at[p, z], gath.at[p, z], s3.at[d], q3.at[d], (peer, n))
            for d, (peer, _) in enumerate(peers)
        ]

    def spread(i, copies):
        gath = blocks[i][6]
        s4, q4 = blocks[i][13:15]
        _, _, p, _, peers = axis_of(i, True)
        for copy in copies:
            copy.wait_recv()
        return [
            send(gath.at[p], gath.at[p], s4.at[d], q4.at[d], (peer, n))
            for d, (peer, _) in enumerate(peers)
        ]

    def adjoint(i, copies):
        for copy in copies:
            copy.wait_recv()
        gath = blocks[i][6]
        wt = [gath[q] for q in range(schemes[i][1])]
        wt = jnp.stack(wt, axis=0 if schemes[i][2] else 1).astype(F32).reshape(cols, tile).astype(BF16)
        for j in range(nj):
            c = lax.dot_general(wt, u[i, j], NT, preferred_element_type=F32)
            c = jnp.where(lanes < ranks_ref[i, j], c, 0.0).astype(BF16)
            b = lax.dot_general(c, v[i, j], NN, preferred_element_type=F32)
            at = slice(j * tile, (j + 1) * tile)
            if i != order[0]:
                b += back[:, at]
            if i != order[-1]:
                back[:, at] = b
                continue
            step = min(width, tile)
            for k in range(tile // step):
                begin = j * tile + k * step
                m, off = begin // width, begin % width
                piece = b[:, k * step : (k + 1) * step]
                back_out[m, :, off : off + step] = piece
                bsend[m, :, off : off + step] = piece.astype(BF16)

    order = list(range(ni))
    steps = (scatter, plane_sum, z_sum, spread, adjoint)
    plan = [(step, i) for step in steps for i in order]
    stage = {}
    for step, i in plan:
        stage[i] = step(i, stage[i]) if i in stage else step(i)

    copies = [
        send(
            bsend.at[peer], brecv.at[d], s5.at[d], q5.at[d], (w, peer)
        )
        for d, peer in enumerate(n_peers)
    ]
    total = back_out[n]
    for d, copy in enumerate(copies):
        copy.wait_recv()
        total += brecv[d].astype(F32)
    adj_ref[...] = total
    for copy in sends:
        copy.wait_send()


def on_device(wide, nn, samples, row_weights, tile_ranks, u_factors, v_factors):
    ni, nj, rank_cap, tile = v_factors.shape
    own_rows, own_cols = samples.shape
    cols = own_rows * nn
    share = cols // wide
    plane = plane_size(wide)
    swapped = (ni // 4,)
    schemes = [
        (plane, wide // plane, True) if i in swapped else (wide // plane, plane, False)
        for i in range(ni)
    ]
    width = own_cols // nn
    dma = pltpu.SemaphoreType.DMA
    vmem = pltpu.VMEM
    some = lambda k: max(k, 1)
    scratch = [
        vmem((nn, own_rows, own_cols), BF16),
        vmem(u_factors.shape, BF16),
        vmem(v_factors.shape, BF16),
        vmem((cols, own_cols), F32),
        vmem((nn, cols, width), BF16),
        vmem((some(nn - 1), cols, width), BF16),
        vmem((nn, cols, width), F32),
        vmem(samples.shape, F32),
        dma(()),
        dma((2, ni)),
        dma((some(nn - 1),)), dma((some(nn - 1),)),
        dma((some(nn - 1),)), dma((some(nn - 1),)),
    ]
    for nz, np_, _ in schemes:
        scratch += [
            vmem((np_, nz, share, tile), F32),
            vmem((np_, nz, share, tile), BF16),
            vmem((some(np_ - 1), nz, share, tile), BF16),
            vmem((nz, share, tile), F32),
            vmem((nz, share, tile), BF16),
            vmem((some(nz - 1), share, tile), BF16),
            vmem((np_, nz, share, tile), BF16),
        ]
        scratch += [dma((some(k - 1),)) for k in (np_, np_, nz, nz, nz, nz, np_, np_)]
    in_vmem = pl.BlockSpec(memory_space=pltpu.VMEM)
    return pl.pallas_call(
        functools.partial(kernel, schemes, nn),
        out_shape=(
            pltpu.VMEM((share, ni * tile), F32),
            pltpu.VMEM((cols, width), F32),
        ),
        in_specs=[
            pl.BlockSpec(memory_space=pltpu.SMEM), in_vmem, pl.BlockSpec(memory_space=pl.ANY),
            pl.BlockSpec(memory_space=pl.ANY), pl.BlockSpec(memory_space=pl.ANY),
        ],
        out_specs=(in_vmem, in_vmem),
        scratch_shapes=scratch,
        compiler_params=pltpu.CompilerParams(
            collective_id=0, has_side_effects=True, vmem_limit_bytes=56 << 20
        ),
        name="operator",
    )(tile_ranks, row_weights, samples, u_factors, v_factors)


def solution(mesh):
    in_specs = (
        P("narrow", "wide"),
        P("narrow"),
        P("narrow", "wide"),
        P("narrow", "wide", None, None),
        P("narrow", "wide", None, None),
    )
    out_specs = (P("wide", "narrow"), P(None, ("wide", "narrow")))
    body = functools.partial(on_device, mesh.shape["wide"], mesh.shape["narrow"])
    return jax.shard_map(
        body, mesh=mesh, in_specs=in_specs, out_specs=out_specs, check_vma=False
    )
```
